32 devices in a mesh: lat: 4 (over y, x), lon: 8 (over z, core).
Axes of the slice: x: 2, y: 2, z: 4, core: 2. Of those that a mesh axis runs over, the one named last changes fastest.
Arguments:
- inputs: float32 [1, 128, 256, 384], P(None, 'lat', 'lon'), may hold values from -6 to 6
- saved: float32 [1, 128, 256, 384], P(None, 'lat', 'lon'), may hold values from -6 to 6
- grad_out: float32 [1, 128, 256, 384], P(None, 'lat', 'lon'), may hold values from -6 to 6
- w_up: float32 [384, 768], replicated, may hold values from -0.3125 to 0.3125
- w_down: float32 [768, 384], replicated, may hold values from -0.21875 to 0.21875
- w_filter: float32 [128, 384, 384], P('lon'), may hold values from -0.3125 to 0.3125
Outputs:
- grad_input: float32 [1, 128, 256, 384], P(None, 'lat', 'lon')
- grad_up: float32 [384, 768], P(None, ('lat', 'lon'))
- grad_down: float32 [768, 384], P(('lat', 'lon'))
- grad_filter: float32 [128, 384, 384], P('lon', 'lat')
The draws below stay inside these ranges and needn't reach their ends.
All inputs are finite; a program needn't handle non-finite values.
Results may differ from the reference program's by a relative error of at most 0.0003.
Values sent between devices are 32-bit elements; how exact they have to be, the bound alone decides.
No kernel may reach another device: no remote copies, remote signals or barrier semaphores. Data moves between devices by JAX's collectives and lax.ppermute only.
A program may use at most 128 MiB of HBM per device.

```python
import math
import jax
import jax.numpy as jnp
from jax import lax

NLAT = 128
NLON = 256
MODES = 128
WIDTH = 384
HIDDEN_SIZE = 768
SAMPLES = 1


def block_levels(stream_key, dims, split, low, high):
    level = 1.0
    for dim, shards_of in split:
        steps = jax.random.uniform(jax.random.fold_in(jax.random.fold_in(stream_key, 6), dim), (shards_of,), jnp.float32, low / len(split), high / len(split))
        level = level * jnp.repeat(jnp.exp(steps), dims[dim] // shards_of).reshape((-1,) + (1,) * (len(dims) - 1 - dim))
    return level


def normal_values(stream_key, shape, scale, limit, pieces=(), kind=jnp.bfloat16):
    drawn = jax.random.normal(stream_key, shape, jnp.float32) * scale
    if len(pieces) > 0:
        drawn = block_levels(stream_key, shape, pieces, -0.22, 0.18) * drawn
    return jnp.clip(drawn, min=-limit, max=limit).astype(kind)


def setup_inputs(seed: int = 0) -> dict:
    splits = jax.random.split(jax.random.key(seed), 7)
    return {
        "inputs": normal_values(splits[0], (SAMPLES, NLAT, NLON, WIDTH), 1.0, 6.0, ((1, 4), (2, 8)), jnp.float32),
        "saved": normal_values(splits[1], (SAMPLES, NLAT, NLON, WIDTH), 1.0, 6.0, ((1, 4), (2, 8)), jnp.float32),
        "grad_out": normal_values(splits[2], (SAMPLES, NLAT, NLON, WIDTH), 1.0, 6.0, ((1, 4), (2, 8)), jnp.float32),
        "w_up": normal_values(splits[3], (WIDTH, HIDDEN_SIZE), WIDTH ** -0.5, 0.3125, (), jnp.float32),
        "w_down": normal_values(splits[4], (HIDDEN_SIZE, WIDTH), HIDDEN_SIZE ** -0.5, 0.21875, (), jnp.float32),
        "w_filter": normal_values(splits[5], (MODES, WIDTH, WIDTH), WIDTH ** -0.5, 0.3125, ((0, 8),), jnp.float32),
    }


HIGHEST = lax.Precision.HIGHEST

def legendre_table(first, count):
    row_ids = jnp.arange(NLAT, dtype=jnp.int32).astype(jnp.float32)
    colatitude = math.pi * (row_ids + 0.5) / NLAT
    cosines = jnp.cos(colatitude)
    sines = jnp.sin(colatitude)
    order_f = (first + jnp.arange(count, dtype=jnp.int32)).astype(jnp.float32)[:, None]
    factor_k = jnp.arange(1, MODES, dtype=jnp.int32).astype(jnp.float32)
    log_prod = jnp.concatenate([jnp.zeros((1,), jnp.float32), jnp.cumsum(jnp.log((2.0 * factor_k - 1.0) / (2.0 * factor_k)))])
    chosen = lax.dynamic_slice_in_dim(log_prod, first, count, 0)
    initial = jnp.exp(0.5 * jnp.log((2.0 * order_f + 1.0) / (4.0 * math.pi)) + 0.5 * chosen[:, None] + order_f * jnp.log(sines)[None, :])

    def advance(carry, degree_f):
        previous, earlier = carry
        scale_a = jnp.sqrt(jnp.maximum(4.0 * degree_f * degree_f - 1.0, 1.0) / jnp.maximum(degree_f * degree_f - order_f * order_f, 1.0))
        below = degree_f - 1.0
        scale_b = jnp.sqrt(jnp.maximum(below * below - order_f * order_f, 0.0) / jnp.maximum(4.0 * below * below - 1.0, 1.0))
        grown = scale_a * (cosines[None, :] * previous - scale_b * earlier)
        current = jnp.where(order_f == degree_f, initial, jnp.where(order_f < degree_f, grown, 0.0))
        return ((current, previous), current)
    zeros = jnp.zeros((count, NLAT), jnp.float32)
    degrees = jnp.arange(MODES, dtype=jnp.int32).astype(jnp.float32)
    _, table = lax.scan(advance, (zeros, zeros), degrees)
    weights = jnp.sqrt(2.0 * math.pi * math.pi * sines / NLAT)
    return jnp.transpose(table, (1, 0, 2)) * weights[None, None, :]

def fourier_table():
    columns = jnp.arange(NLON, dtype=jnp.int32)
    orders = jnp.arange(MODES, dtype=jnp.int32)
    phase = columns[:, None] * orders[None, :] % NLON
    angle = 2.0 * math.pi * phase.astype(jnp.float32) / NLON
    return jnp.concatenate([jnp.cos(angle), -jnp.sin(angle)], axis=1) * math.sqrt(2.0 / NLON)

def analysis(field, legendre, fourier):
    count = field.shape[0]
    spectra_lon = jnp.einsum('bjkc,kq->bjqc', field, fourier, precision=HIGHEST)
    spectra_lon = spectra_lon.reshape(count, NLAT, 2, MODES, WIDTH)
    return jnp.einsum('mlj,bjpmc->bpmlc', legendre, spectra_lon, precision=HIGHEST)

def synthesis(coeffs, legendre, fourier):
    count = coeffs.shape[0]
    columns = jnp.einsum('mlj,bpmlc->bjpmc', legendre, coeffs, precision=HIGHEST)
    columns = columns.reshape(count, NLAT, 2 * MODES, WIDTH)
    return jnp.einsum('bjqc,kq->bjkc', columns, fourier, precision=HIGHEST)

def gelu_tanh(values):
    return jax.nn.gelu(values, approximate=True)

def reference(inputs, saved, grad_out, w_up, w_down, w_filter):
    flat_grad = grad_out.reshape(-1, WIDTH)
    flat_saved = saved.reshape(-1, WIDTH)
    preact = jnp.dot(flat_saved, w_up, precision=HIGHEST, preferred_element_type=jnp.float32)
    activated, gelu_back = jax.vjp(gelu_tanh, preact)
    grad_act = jnp.dot(flat_grad, w_down.T, precision=HIGHEST, preferred_element_type=jnp.float32)
    grad_pre = gelu_back(grad_act)[0]
    grad_flat = flat_grad + jnp.dot(grad_pre, w_up.T, precision=HIGHEST, preferred_element_type=jnp.float32)
    point_scale = 1.0 / math.sqrt(SAMPLES * NLAT * NLON)
    grad_up = jnp.dot(flat_saved.T, grad_pre, precision=HIGHEST, preferred_element_type=jnp.float32) * point_scale
    grad_down = jnp.dot(activated.T, flat_grad, precision=HIGHEST, preferred_element_type=jnp.float32) * point_scale
    grad_field = grad_flat.reshape(grad_out.shape)
    legendre = legendre_table(0, MODES)
    fourier = fourier_table()
    spectra = analysis(inputs, legendre, fourier)
    grad_spec = analysis(grad_field, legendre, fourier)
    grad_coef = jnp.einsum('bpmld,lcd->bpmlc', grad_spec, w_filter, precision=HIGHEST)
    grad_filter = jnp.einsum('bpmlc,bpmld->lcd', spectra, grad_spec, precision=HIGHEST) / math.sqrt(2.0 * SAMPLES * MODES)
    grad_input = grad_field + synthesis(grad_coef, legendre, fourier)
    return (grad_input, grad_up, grad_down, grad_filter)
```

```python
import functools
import math

import jax
import jax.numpy as jnp
from jax import lax
from jax.experimental import pallas as pl
from jax.experimental.pallas import tpu as pltpu
from jax.sharding import PartitionSpec as P

LANES = 128
F32 = jnp.float32
BF16 = jnp.bfloat16
HIGH = lax.Precision.HIGH


def split(x):
    hi = x.astype(BF16)
    return hi, (x - hi.astype(F32)).astype(BF16)


def dot(x, y):
    return lax.dot_general(x, y, (((1,), (0,)), ((), ())), preferred_element_type=F32)


def dot_nt(x, y):
    return lax.dot_general(x, y, (((1,), (1,)), ((), ())), preferred_element_type=F32)


def call(kernel, flops=0, **kwargs):
    outs = kwargs["out_shape"]
    outs = outs if isinstance(outs, (list, tuple)) else [outs]
    size = sum(math.prod(o.shape) * o.dtype.itemsize for o in outs)
    return pl.pallas_call(
        kernel,
        cost_estimate=pl.CostEstimate(flops=flops, bytes_accessed=3 * size, transcendentals=0),
        compiler_params=pltpu.CompilerParams(vmem_limit_bytes=60 * 1024 * 1024),
        **kwargs,
    )


def fourier_columns(nlon_pts, modes, nlat, per):
    shape = (nlon_pts, 2 * nlat * LANES)
    col = lax.broadcasted_iota(jnp.int32, shape, 1)
    k = lax.broadcasted_iota(jnp.int32, shape, 0)
    order = (col // (2 * LANES)) * per + col % per
    part = (col // LANES) % 2
    phase = (k * order + part * (nlon_pts // 4)) % nlon_pts
    return jnp.cos(2.0 * math.pi * phase.astype(F32) / nlon_pts) * math.sqrt(2.0 / nlon_pts)


def block_table_kernel(per, f_ref, hi_ref, lo_ref):
    reps = LANES // per
    shape = (per, f_ref.shape[1])
    which = (lax.broadcasted_iota(jnp.int32, shape, 1) % LANES) // per
    values = f_ref[...]
    for i in range(reps):
        hi, lo = split(jnp.where(which == i, values, 0.0))
        hi_ref[i * per : (i + 1) * per, :] = hi
        lo_ref[i * per : (i + 1) * per, :] = lo


def block_table(f, per):
    blocks = f.shape[0] // per
    cols = f.shape[1]
    out = jax.ShapeDtypeStruct((blocks * LANES, cols), BF16)
    return call(
        functools.partial(block_table_kernel, per),
        out_shape=(out, out),
        grid=(blocks,),
        in_specs=[pl.BlockSpec((per, cols), lambda i: (i, 0))],
        out_specs=[pl.BlockSpec((LANES, cols), lambda i: (i, 0))] * 2,
    )(f)


def legendre_kernel(nlat_pts, modes, first_ref, hi_ref, lo_ref, thi_ref, tlo_ref, scr):
    count = hi_ref.shape[0] // modes
    shape = (count, nlat_pts)
    rows = lax.broadcasted_iota(jnp.int32, shape, 1).astype(F32)
    theta = math.pi * (rows + 0.5) / nlat_pts
    cosines = jnp.cos(theta)
    sines = jnp.sin(theta)
    weights = jnp.sqrt(2.0 * math.pi * math.pi * sines / nlat_pts)
    order = (first_ref[0] + lax.broadcasted_iota(jnp.int32, shape, 0)).astype(F32)
    kshape = (count, modes)
    k = lax.broadcasted_iota(jnp.int32, kshape, 1).astype(F32)
    order_k = (first_ref[0] + lax.broadcasted_iota(jnp.int32, kshape, 0)).astype(F32)
    safe = jnp.maximum(k, 1.0)
    logs = jnp.where((k >= 1.0) & (k <= order_k), jnp.log((2.0 * safe - 1.0) / (2.0 * safe)), 0.0)
    log_prod = jnp.sum(logs, axis=1, keepdims=True)
    initial = jnp.exp(
        0.5 * jnp.log((2.0 * order + 1.0) / (4.0 * math.pi))
        + 0.5 * log_prod
        + order * jnp.log(sines)
    )
    square = order * order

    def advance(step, carry):
        previous, earlier = carry
        degree = lax.convert_element_type(step, F32)
        below = degree - 1.0
        scale_a = jnp.sqrt(
            jnp.maximum(4.0 * degree * degree - 1.0, 1.0)
            / jnp.maximum(degree * degree - square, 1.0)
        )
        scale_b = jnp.sqrt(
            jnp.maximum(below * below - square, 0.0)
            / jnp.maximum(4.0 * below * below - 1.0, 1.0)
        )
        grown = scale_a * (cosines * previous - scale_b * earlier)
        current = jnp.where(order == degree, initial, jnp.where(order < degree, grown, 0.0))
        scr[pl.ds(step, count, stride=modes), :] = current * weights
        return current, previous

    zeros = jnp.where(order < 0.0, initial, 0.0)
    lax.fori_loop(0, modes, advance, (zeros, zeros), unroll=4)

    def convert(m, _):
        at = pl.ds(pl.multiple_of(m * modes, modes), modes)
        block = scr[at, :]
        hi, lo = split(block)
        hi_ref[at, :] = hi
        lo_ref[at, :] = lo
        att = pl.ds(pl.multiple_of(m * nlat_pts, nlat_pts), nlat_pts)
        hi, lo = split(block.T)
        thi_ref[att, :] = hi
        tlo_ref[att, :] = lo
        return 0

    lax.fori_loop(0, count, convert, 0, unroll=2)


def legendre_tables(first, count, nlat_pts, modes):
    a = jax.ShapeDtypeStruct((count * modes, nlat_pts), BF16)
    b = jax.ShapeDtypeStruct((count * nlat_pts, modes), BF16)
    return call(
        functools.partial(legendre_kernel, nlat_pts, modes),
        out_shape=(a, a, b, b),
        in_specs=[pl.BlockSpec(memory_space=pltpu.SMEM)],
        scratch_shapes=[pltpu.VMEM((count * modes, nlat_pts), F32)],
    )(first)


def to_rows_kernel(x_ref, o_ref):
    turned = x_ref[...].T
    o_ref[:, 0] = turned.reshape(o_ref.shape[0], o_ref.shape[2], LANES)


def to_rows(flat, nlon):
    rows, width = flat.shape
    groups = rows // LANES
    return call(
        to_rows_kernel,
        out_shape=jax.ShapeDtypeStruct((nlon, groups, width // nlon, LANES), F32),
        grid=(groups,),
        in_specs=[pl.BlockSpec((LANES, width), lambda g: (g, 0))],
        out_specs=pl.BlockSpec((nlon, 1, width // nlon, LANES), lambda g: (0, g, 0, 0)),
    )(flat)


def from_rows_kernel(x_ref, add_ref, o_ref):
    block = x_ref[:, 0].reshape(-1, LANES)
    o_ref[...] = add_ref[...] + block.T


def from_rows(x, add):
    nlon, groups, per, _ = x.shape
    width = nlon * per
    return call(
        from_rows_kernel,
        out_shape=jax.ShapeDtypeStruct(add.shape, F32),
        grid=(groups,),
        in_specs=[
            pl.BlockSpec((nlon, 1, per, LANES), lambda g: (0, g, 0, 0)),
            pl.BlockSpec((LANES, width), lambda g: (g, 0)),
        ],
        out_specs=pl.BlockSpec((LANES, width), lambda g: (g, 0)),
    )(x, add)


def fourier_kernel(x_ref, hi_ref, lo_ref, o_ref, xhi, xlo):
    blocks, groups, per, _ = x_ref.shape

    @pl.when(pl.program_id(0) == 0)
    def _():
        for r in range(blocks):
            hi, lo = split(x_ref[r].reshape(groups * per, LANES))
            xhi[:, r * LANES : (r + 1) * LANES] = hi
            xlo[:, r * LANES : (r + 1) * LANES] = lo

    y = dot(xhi[...], hi_ref[...]) + dot(xhi[...], lo_ref[...]) + dot(xlo[...], hi_ref[...])
    for p in range(2):
        o_ref[0, :, p] = y[:, p * LANES : (p + 1) * LANES].reshape(groups, per, LANES)


def fourier(x, table, nlat):
    blocks, groups, per, _ = x.shape
    deep = blocks * LANES
    rows = groups * per
    return call(
        fourier_kernel,
        flops=2 * rows * deep * nlat * 2 * LANES * 3,
        out_shape=jax.ShapeDtypeStruct((nlat, groups, 2, per, LANES), F32),
        grid=(nlat,),
        in_specs=[
            pl.BlockSpec(x.shape, lambda a: (0, 0, 0, 0)),
            pl.BlockSpec((deep, 2 * LANES), lambda a: (0, a)),
            pl.BlockSpec((deep, 2 * LANES), lambda a: (0, a)),
        ],
        out_specs=pl.BlockSpec((1, groups, 2, per, LANES), lambda a: (a, 0, 0, 0, 0)),
        scratch_shapes=[pltpu.VMEM((rows, deep), BF16)] * 2,
    )(x, *table)


def unfourier_kernel(x_ref, hi_ref, lo_ref, o_ref, xhi, xlo):
    nlat, groups, _, per, _ = x_ref.shape

    @pl.when(pl.program_id(0) == 0)
    def _():
        for a in range(nlat):
            for p in range(2):
                at = (2 * a + p) * LANES
                hi, lo = split(x_ref[a, :, p].reshape(groups * per, LANES))
                xhi[:, at : at + LANES] = hi
                xlo[:, at : at + LANES] = lo

    y = (
        dot_nt(xhi[...], hi_ref[...])
        + dot_nt(xhi[...], lo_ref[...])
        + dot_nt(xlo[...], hi_ref[...])
    )
    for r in range(o_ref.shape[0]):
        o_ref[r] = y[:, r * LANES : (r + 1) * LANES].reshape(groups, per, LANES)


def unfourier(x, table, nlon):
    nlat, groups, _, per, _ = x.shape
    deep = nlat * 2 * LANES
    rows = groups * per
    return call(
        unfourier_kernel,
        flops=2 * rows * deep * nlon * LANES * 3,
        out_shape=jax.ShapeDtypeStruct((nlon, groups, per, LANES), F32),
        grid=(nlon // 2,),
        in_specs=[
            pl.BlockSpec(x.shape, lambda r: (0, 0, 0, 0, 0)),
            pl.BlockSpec((2 * LANES, deep), lambda r: (r, 0)),
            pl.BlockSpec((2 * LANES, deep), lambda r: (r, 0)),
        ],
        out_specs=pl.BlockSpec((2, groups, per, LANES), lambda r: (r, 0, 0, 0)),
        scratch_shapes=[pltpu.VMEM((rows, deep), BF16)] * 2,
    )(x, *table)


def legendre_sum_kernel(count, x_ref, hi_ref, lo_ref, o_ref, v, w):
    groups = x_ref.shape[0]
    outs = o_ref.shape[0]
    rows = x_ref.shape[1]
    deep = groups * LANES // count
    wide = outs * LANES // count

    def enter(g, _):
        at = pl.ds(pl.multiple_of(g * LANES, LANES), LANES)
        v[at, :rows] = x_ref[g].T
        return 0

    lax.fori_loop(0, groups, enter, 0, unroll=2)

    def order(m, _):
        xhi, xlo = split(v[pl.ds(m, deep, stride=count), :])
        at = pl.ds(pl.multiple_of(m * wide, wide), wide)
        thi = hi_ref[at, :]
        w[pl.ds(m, wide, stride=count), :] = dot(thi, xhi) + dot(thi, xlo) + dot(lo_ref[at, :], xhi)
        return 0

    lax.fori_loop(0, count, order, 0, unroll=4)

    def leave(g, _):
        at = pl.ds(pl.multiple_of(g * LANES, LANES), LANES)
        o_ref[g] = w[at, :].T[:rows]
        return 0

    lax.fori_loop(0, outs, leave, 0, unroll=2)


def legendre_sum(x, table, count):
    wide = table[0].shape[0] // count
    outs = wide * count // LANES
    groups, rows, _ = x.shape
    return call(
        functools.partial(legendre_sum_kernel, count),
        flops=2 * count * wide * table[0].shape[1] * rows * 3,
        out_shape=jax.ShapeDtypeStruct((outs, rows, LANES), F32),
        scratch_shapes=[
            pltpu.VMEM((groups * LANES, LANES), F32),
            pltpu.VMEM((outs * LANES, LANES), F32),
        ],
    )(x, *table)


def lane_degree(shape, count):
    return (lax.broadcasted_iota(jnp.int32, shape, 1) % LANES) // count


def degree_matrix(ref):
    halves = [ref[:, 0, p].reshape(-1, LANES) for p in range(2)]
    return jnp.concatenate(halves, axis=1)


def filter_kernel(count, g_ref, w_ref, o_ref):
    nlon, _, _, per, _ = g_ref.shape
    ghi, glo = split(degree_matrix(g_ref))
    degree = lane_degree(ghi.shape, count)
    total = jnp.zeros(ghi.shape, F32)
    for i in range(w_ref.shape[0]):
        whi, wlo = split(w_ref[i])
        y = dot(whi, ghi) + dot(whi, glo) + dot(wlo, ghi)
        total = jnp.where(degree == i, y, total)
    for p in range(2):
        o_ref[:, 0, p] = total[:, p * LANES : (p + 1) * LANES].reshape(nlon, per, LANES)


def apply_filter(g, w, count):
    nlon, groups, _, per, _ = g.shape
    width = nlon * per
    step = LANES // count
    block = pl.BlockSpec((nlon, 1, 2, per, LANES), lambda i: (0, i, 0, 0, 0))
    return call(
        functools.partial(filter_kernel, count),
        flops=2 * w.size * 2 * LANES * 3,
        out_shape=jax.ShapeDtypeStruct(g.shape, F32),
        grid=(groups,),
        in_specs=[block, pl.BlockSpec((step, width, width), lambda i: (i, 0, 0))],
        out_specs=block,
    )(g, w)


def filter_grad_kernel(count, scale, s_ref, g_ref, o_ref):
    s = degree_matrix(s_ref) * scale
    ghi, glo = split(degree_matrix(g_ref).T)
    degree = lane_degree(s.shape, count)
    for i in range(o_ref.shape[0]):
        shi, slo = split(jnp.where(degree == i, s, 0.0))
        o_ref[i] = dot(shi, ghi) + dot(shi, glo) + dot(slo, ghi)


def filter_grad(s, g, count, scale):
    nlon, groups, _, per, _ = g.shape
    width = nlon * per
    step = LANES // count
    block = pl.BlockSpec((nlon, 1, 2, per, LANES), lambda i: (0, i, 0, 0, 0))
    return call(
        functools.partial(filter_grad_kernel, count, scale),
        flops=2 * groups * step * width * width * 2 * LANES * 3,
        out_shape=jax.ShapeDtypeStruct((groups * step, width, width), F32),
        grid=(groups,),
        in_specs=[block, block],
        out_specs=pl.BlockSpec((step, width, width), lambda i: (i, 0, 0)),
    )(s, g)


def exchange(x, axis):
    return lax.all_to_all(x, axis, split_axis=0, concat_axis=0, tiled=True)


def gelu_tanh(values):
    return jax.nn.gelu(values, approximate=True)


def shards(inputs, saved, grad_out, w_up, w_down, w_filter):
    nlat, nlon = lax.axis_size("lat"), lax.axis_size("lon")
    samples, lat_rows, lon_cols, width = inputs.shape
    nlat_pts, nlon_pts = nlat * lat_rows, nlon * lon_cols
    modes = w_filter.shape[0] * nlon
    count = modes // nlat
    hidden = w_up.shape[1]
    deg = w_filter.shape[0] * count // LANES

    table = block_table(fourier_columns(nlon_pts, modes, nlat, count), lon_cols)
    first = (lax.axis_index("lat") * count).astype(jnp.int32).reshape(1)
    lhi, llo, lthi, ltlo = legendre_tables(first, count, nlat_pts, modes)

    def analysis(flat):
        rows = exchange(to_rows(flat, nlon), "lon")
        by_order = exchange(fourier(rows, table, nlat), "lat")
        per = 2 * (width // nlon)
        coeffs = legendre_sum(by_order.reshape(-1, per, LANES), (lhi, llo), count)
        return exchange(coeffs.reshape(nlon, deg, 2, per // 2, LANES), "lon")

    flat_grad = grad_out.reshape(-1, width)
    flat_saved = saved.reshape(-1, width)
    preact = jnp.dot(flat_saved, w_up, precision=HIGH, preferred_element_type=F32)
    activated, gelu_back = jax.vjp(gelu_tanh, preact)
    grad_act = jnp.dot(flat_grad, w_down.T, precision=HIGH, preferred_element_type=F32)
    grad_pre = gelu_back(grad_act)[0]
    grad_flat = flat_grad + jnp.dot(grad_pre, w_up.T, precision=HIGH, preferred_element_type=F32)

    grad_spec = analysis(grad_flat)
    spectra = analysis(inputs.reshape(-1, width))

    point_scale = 1.0 / math.sqrt(samples * nlat_pts * nlon_pts)
    part_up = jnp.dot(grad_pre.T, flat_saved, precision=HIGH, preferred_element_type=F32)
    part_down = jnp.dot(activated.T, flat_grad, precision=HIGH, preferred_element_type=F32)
    parts = jnp.concatenate([part_up, part_down], axis=1) * point_scale
    summed = lax.psum_scatter(parts, ("lat", "lon"), scatter_dimension=0, tiled=True)
    grad_up = summed[:, :width].T
    grad_down = summed[:, width:]

    filter_scale = 1.0 / math.sqrt(2.0 * samples * modes)
    partial = filter_grad(spectra, grad_spec, count, filter_scale)
    grad_filter = lax.psum_scatter(partial, "lat", scatter_dimension=1, tiled=True)

    grad_coef = exchange(apply_filter(grad_spec, w_filter, count), "lon")
    per = 2 * (width // nlon)
    columns = legendre_sum(grad_coef.reshape(-1, per, LANES), (lthi, ltlo), count)
    groups = columns.shape[0] // nlat
    by_row = exchange(columns.reshape(nlat, groups, 2, per // 2, LANES), "lat")
    gridded = exchange(unfourier(by_row, table, nlon), "lon")
    grad_input = from_rows(gridded, grad_flat).reshape(inputs.shape)
    return (grad_input, grad_up, grad_down, grad_filter)


def solution(mesh):
    in_specs = (
        P(None, "lat", "lon", None),
        P(None, "lat", "lon", None),
        P(None, "lat", "lon", None),
        P(),
        P(),
        P("lon", None, None),
    )
    out_specs = (
        P(None, "lat", "lon", None),
        P(None, ("lat", "lon")),
        P(("lat", "lon"), None),
        P("lon", "lat", None),
    )
    return jax.shard_map(shards, mesh=mesh, in_specs=in_specs, out_specs=out_specs, check_vma=False)
```
